128 devices in a mesh: sta: 64 (over x, y, z_hi, core), per: 2 (over z_lo).
Axes of the slice: x: 4, y: 4, z: 4 (z_hi: 2, z_lo: 2; z = z_hi * 2 + z_lo), core: 2. Of those that a mesh axis runs over, the one named last changes fastest.
Arguments:
- spectra: bfloat16 [1024, 2, 8192], P('sta', None, 'per'), may hold values from -6 to 6
- pick_bins: int32 [8, 1024, 48], P(None, ('sta', 'per')), may hold values from 0 to 127
- path_cells: int32 [1024, 2, 48], P(('sta', 'per')), may hold values from 0 to 8191
Outputs:
- helmholtz: float32 [8, 64, 128], P('per', 'sta')
The draws below stay inside these ranges and needn't reach their ends.
All inputs are finite; a program needn't handle non-finite values.
Results may differ from the reference program's by a relative error of at most 0.0042.
Values may be sent and summed in bfloat16 or wider, within the bound.
A program may use at most 64 MiB of HBM per device.

```python
import math
import jax
import jax.numpy as jnp
from jax import lax

FREQ = 8192
NLAG = 128
PERIODS = 8
OFFS = 3
S_DEV = 16
MAP_COLS = 128
STATIONS = 1024
PAIR_COLS = 48
MAP_ROWS = 64
CELLS = 8192
N_STA = 64


def plant(values, rng, least, top_value):
    dims = values.shape
    place = [jax.random.randint(jax.random.fold_in(rng, axis), (), 0, dims[axis]) for axis in range(len(dims))]
    values = values.at[tuple(place)].set(least)
    longest = dims.index(max(dims))
    place[longest] = (place[longest] + 1) % dims[longest]
    return values.at[tuple(place)].set(top_value)


def block_scale(stream_key, extent, pieces, smallest, top_value):
    loudness = 1.0
    for axis_at, shards_of in pieces:
        draws = jax.random.uniform(jax.random.fold_in(jax.random.fold_in(stream_key, 6), axis_at), (shards_of,), jnp.float32, smallest / len(pieces), top_value / len(pieces))
        loudness = loudness * jnp.repeat(jnp.exp(draws), extent[axis_at] // shards_of).reshape((-1,) + (1,) * (len(extent) - 1 - axis_at))
    return loudness


def gaussian(stream_key, shape, deviation, reach, shards=(), held_as=jnp.bfloat16):
    drawn = deviation * jax.random.normal(stream_key, shape, jnp.float32)
    if shards:
        drawn = drawn * block_scale(stream_key, shape, shards, -0.22, 0.18)
    return jnp.clip(drawn, -reach, reach).astype(held_as)


def setup_inputs(seed: int = 0) -> dict:
    seeds = jax.random.split(jax.random.key(seed), 4)
    spectra = gaussian(seeds[0], (STATIONS, 2, FREQ), 1.0, 6.0, ((0, 64), (2, 2)))
    pick_bins = plant(jax.random.randint(seeds[1], (PERIODS, STATIONS, PAIR_COLS), 0, NLAG), jax.random.fold_in(seeds[1], 1), 0, NLAG - 1).astype(jnp.int32)
    path_cells = plant(jax.random.randint(seeds[2], (STATIONS, 2, PAIR_COLS), 0, CELLS), jax.random.fold_in(seeds[2], 1), 0, CELLS - 1).astype(jnp.int32)
    return {"spectra": spectra, "pick_bins": pick_bins, "path_cells": path_cells}


def lag_table(first_bin, bin_count, lag_count, total_bins):
    freq_index = (first_bin + jnp.arange(bin_count, dtype=jnp.int32))[:, None]
    lag_index = jnp.arange(lag_count, dtype=jnp.int32)[None, :] - lag_count // 2
    turned = (freq_index * lag_index) % (2 * total_bins)
    phase = turned.astype(jnp.float32) * (math.pi / total_bins)
    scale = total_bins ** -0.5
    return jnp.stack([jnp.cos(phase) * scale, -jnp.sin(phase) * scale]).astype(jnp.bfloat16)


def cross_block(resident, visiting, table_part):
    resident_re = resident[:, 0].astype(jnp.float32)[:, None, :]
    resident_im = resident[:, 1].astype(jnp.float32)[:, None, :]
    visiting_re = visiting[:, 0].astype(jnp.float32)[None, :, :]
    visiting_im = visiting[:, 1].astype(jnp.float32)[None, :, :]
    cross_re = (resident_re * visiting_re + resident_im * visiting_im).astype(jnp.bfloat16)
    cross_im = (resident_im * visiting_re - resident_re * visiting_im).astype(jnp.bfloat16)
    stacked = jnp.stack([cross_re, cross_im], axis=2)
    pair_rows = stacked.shape[0] * stacked.shape[1]
    return jnp.dot(stacked.reshape(pair_rows, -1), table_part.reshape(-1, table_part.shape[-1]),
                   preferred_element_type=jnp.float32)


def reference(spectra, pick_bins, path_cells):
    blocks = spectra.reshape(N_STA, S_DEV, 2, FREQ)
    cos_table = lag_table(0, FREQ, NLAG, FREQ)
    not_self = 1.0 - jnp.eye(S_DEV, dtype=jnp.float32)

    def one_block(block_index):
        resident = blocks[block_index]
        panels = []
        for offset in range(OFFS):
            visiting = blocks[(block_index - offset) % N_STA]
            panel = cross_block(resident, visiting, cos_table).reshape(S_DEV, S_DEV, NLAG)
            if offset == 0:
                panel = panel * not_self[:, :, None]
            panels.append(panel)
        return jnp.stack(panels, axis=1).reshape(S_DEV, OFFS * S_DEV, NLAG)

    correlations = lax.map(one_block, jnp.arange(N_STA, dtype=jnp.int32))
    correlations = correlations.reshape(STATIONS, OFFS * S_DEV, NLAG)
    picked = jnp.take_along_axis(correlations, jnp.transpose(pick_bins, (1, 2, 0)), axis=2)
    picked = jnp.transpose(picked, (2, 0, 1))
    spread = jnp.broadcast_to(picked[:, :, None, :], (PERIODS, STATIONS, 2, OFFS * S_DEV)).reshape(PERIODS, -1)
    flat_cells = path_cells.reshape(-1)
    time_field = jnp.zeros((PERIODS, CELLS), jnp.float32).at[:, flat_cells].add(spread)
    energy = jnp.zeros((PERIODS, CELLS), jnp.float32).at[:, flat_cells].add(spread * spread)
    field_u = jnp.pad(time_field.reshape(PERIODS, MAP_ROWS, MAP_COLS), ((0, 0), (1, 1), (1, 1)))
    amplitude = 1.0 + jnp.pad(energy.reshape(PERIODS, MAP_ROWS, MAP_COLS), ((0, 0), (1, 1), (1, 1)))
    grad_rows = (field_u[:, 2:, 1:-1] - field_u[:, :-2, 1:-1]) * 0.5
    grad_cols = (field_u[:, 1:-1, 2:] - field_u[:, 1:-1, :-2]) * 0.5
    centre = amplitude[:, 1:-1, 1:-1]
    laplace = (amplitude[:, 2:, 1:-1] + amplitude[:, :-2, 1:-1] + amplitude[:, 1:-1, 2:]
               + amplitude[:, 1:-1, :-2] - 4.0 * centre)
    weight = 1.0 / (1.0 + jnp.arange(PERIODS, dtype=jnp.int32).astype(jnp.float32))
    return grad_rows * grad_rows + grad_cols * grad_cols - weight[:, None, None] * laplace / centre
```

```python
import functools
import math

import jax
import jax.numpy as jnp
import numpy as np
from jax import lax
from jax.experimental import pallas as pl
from jax.experimental.pallas import tpu as pltpu
from jax.sharding import PartitionSpec as P

FREQ = 8192
NLAG = 128
COARSE = 128
MESH = pl.DeviceIdType.MESH


def angle_tables(per_count):
    lag = np.arange(NLAG, dtype=np.int64) - NLAG // 2
    coarse = np.arange(FREQ // COARSE, dtype=np.int64) * COARSE
    fine = np.arange(COARSE, dtype=np.int64)
    out = []
    for bins, scale in ((coarse, FREQ ** -0.5), (fine, 1.0)):
        turned = (bins[:, None] * lag[None, :]) % (2 * FREQ)
        phase = turned.astype(np.float64) * (math.pi / FREQ)
        out.append(np.stack([np.cos(phase), np.sin(phase)]).astype(np.float32) * np.float32(scale))
    coarse_table, fine_table = out
    coarse_table = coarse_table.reshape(2, per_count, -1, NLAG).transpose(1, 0, 2, 3)
    return coarse_table, fine_table


def build_table(coarse_ref, fine_ref, table_ref, per_place):
    band = table_ref.shape[1]

    def one(step, carry):
        c = coarse_ref[per_place, 0, pl.ds(step, 1), :]
        s = coarse_ref[per_place, 1, pl.ds(step, 1), :]
        rows = pl.ds(pl.multiple_of(step * COARSE, COARSE), COARSE)
        fc = fine_ref[0]
        fs = fine_ref[1]
        table_ref[0, rows, :] = (c * fc - s * fs).astype(jnp.bfloat16)
        table_ref[1, rows, :] = (-(s * fc + c * fs)).astype(jnp.bfloat16)
        return carry

    lax.fori_loop(0, band // COARSE, one, 0)


def correlate_into(acc_refs, res_ref, vis_refs, table_ref, chunk):
    count = res_ref.shape[1]
    band = res_ref.shape[2]
    for acc in acc_refs:
        acc[...] = jnp.zeros_like(acc)

    def one(step, carry):
        cols = pl.ds(pl.multiple_of(step * chunk, chunk), chunk)
        cos_part = table_ref[0, cols, :]
        sin_part = table_ref[1, cols, :]
        rre = res_ref[0, :, cols].astype(jnp.float32)
        rim = res_ref[1, :, cols].astype(jnp.float32)
        for acc, vis in zip(acc_refs, vis_refs):
            vre = vis[0, :, cols].astype(jnp.float32)
            vim = vis[1, :, cols].astype(jnp.float32)
            res, ims = [], []
            for i in range(count):
                a = rre[i:i + 1]
                b = rim[i:i + 1]
                res.append((a * vre + b * vim).astype(jnp.bfloat16))
                ims.append((b * vre - a * vim).astype(jnp.bfloat16))
            cre = jnp.concatenate(res, axis=0)
            cim = jnp.concatenate(ims, axis=0)
            acc[...] += jnp.dot(cre, cos_part, preferred_element_type=jnp.float32) + jnp.dot(
                cim, sin_part, preferred_element_type=jnp.float32
            )
        return carry

    lax.fori_loop(0, band // chunk, one, 0)


def own_kernel(res_ref, coarse_ref, fine_ref, table_ref, corr_ref):
    per_place = lax.axis_index("per")
    build_table(coarse_ref, fine_ref, table_ref, per_place)
    correlate_into([corr_ref], res_ref, [res_ref], table_ref, 512)


def visit_kernel(res_ref, near_ref, far_ref, table_ref, corr_ref, bins_ref, picks_ref, acc_near, acc_far):
    correlate_into([acc_near, acc_far], res_ref, [near_ref, far_ref], table_ref, 512)
    pairs = corr_ref.shape[0]
    periods = bins_ref.shape[0]
    half = periods // 2
    lag = lax.broadcasted_iota(jnp.int32, (NLAG, pairs), 0)
    for k, acc in enumerate((corr_ref, acc_near, acc_far)):
        turned = acc[...].T
        rows = []
        for p in range(periods):
            wanted = bins_ref[p:p + 1, k * pairs:(k + 1) * pairs]
            rows.append(jnp.sum(jnp.where(lag == wanted, turned, 0.0), axis=0, keepdims=True))
        got = jnp.concatenate(rows, axis=0)
        if k == 0:
            side = int(math.isqrt(pairs))
            place = lax.broadcasted_iota(jnp.int32, (periods, pairs), 1)
            got = jnp.where(place // side == place % side, 0.0, got)
        picks_ref[0, :, k * pairs:(k + 1) * pairs] = got[:half]
        picks_ref[1, :, k * pairs:(k + 1) * pairs] = got[half:]


def map_kernel(sta_count, picks_ref, cells_ref, out_ref, peer_picks, spread, landed, edge_own, edges,
               lhs, pick_sems, send_sem, recv_sem, edge_send, edge_recv):
    sta = lax.axis_index("sta")
    per = lax.axis_index("per")
    others = sta_count - 1
    barrier = pltpu.get_barrier_semaphore()
    pl.semaphore_signal(barrier, inc=1, device_id=(sta, 1 - per), device_id_type=MESH)

    def greet(step, carry):
        there = lax.rem(sta + step, sta_count)
        pl.semaphore_signal(barrier, inc=1, device_id=(there, per), device_id_type=MESH)
        return carry

    lax.fori_loop(1, sta_count, greet, 0)
    pl.semaphore_wait(barrier, sta_count)

    trade = pltpu.make_async_remote_copy(
        src_ref=picks_ref.at[1 - per], dst_ref=peer_picks, send_sem=pick_sems.at[0], recv_sem=pick_sems.at[1],
        device_id=(sta, 1 - per), device_id_type=MESH)
    trade.start()
    cell = cells_ref[...]
    ends = cell.shape[1]
    col = cell % 128
    row = cell // 128
    col_hot = (lax.broadcasted_iota(jnp.int32, (128, ends), 0) == col).astype(jnp.bfloat16)
    trade.wait()
    total = picks_ref[per] + peer_picks[...]
    both = jnp.concatenate([total, total * total], axis=0)
    high = both.astype(jnp.bfloat16).astype(jnp.float32)
    low = both - high
    vals = jnp.concatenate([high, low], axis=0)
    vals = jnp.concatenate([vals, vals], axis=1)

    for r in range(sta_count):
        lhs[r * 16:(r + 1) * 16, :] = jnp.where(row == r, vals, 0.0).astype(jnp.bfloat16)
    grid = lax.dot_general(lhs[...], col_hot, (((1,), (1,)), ((), ())), preferred_element_type=jnp.float32)
    grid = grid.reshape(sta_count, 2, 8, 128)
    spread[...] = grid[:, 0] + grid[:, 1]

    def send(step, carry):
        there = lax.rem(sta + step, sta_count)
        pltpu.make_async_remote_copy(
            src_ref=spread.at[there], dst_ref=landed.at[step - 1], send_sem=send_sem, recv_sem=recv_sem,
            device_id=(there, per), device_id_type=MESH).start()
        return carry

    lax.fori_loop(1, sta_count, send, 0)
    pltpu.make_async_copy(landed, landed, recv_sem).wait()
    edge_own[...] = spread[sta] + jnp.sum(landed[...], axis=0)
    copies = []
    for side, step in enumerate((1, sta_count - 1)):
        there = lax.rem(sta + step, sta_count)
        copy = pltpu.make_async_remote_copy(
            src_ref=edge_own, dst_ref=edges.at[side], send_sem=edge_send.at[side], recv_sem=edge_recv.at[side],
            device_id=(there, per), device_id_type=MESH)
        copy.start()
        copies.append(copy)
    own = edge_own[...]
    half = own.shape[0] // 2
    lane = lax.broadcasted_iota(jnp.int32, own.shape, 1)
    before_col = jnp.where(lane == 0, 0.0, pltpu.roll(own, 1, 1))
    after_col = jnp.where(lane == 127, 0.0, pltpu.roll(own, 127, 1))
    for copy in copies:
        copy.wait()
    before = jnp.where(sta == 0, 0.0, edges[0])
    after = jnp.where(sta == sta_count - 1, 0.0, edges[1])
    grad_rows = (after[:half] - before[:half]) * 0.5
    grad_cols = (after_col[:half] - before_col[:half]) * 0.5
    amp = 1.0 + own[half:]
    laplace = ((1.0 + after[half:]) + (1.0 + before[half:]) + (1.0 + after_col[half:])
               + (1.0 + before_col[half:]) - 4.0 * amp)
    period = per * half + lax.broadcasted_iota(jnp.int32, laplace.shape, 0)
    weight = 1.0 / (1.0 + period.astype(jnp.float32))
    result = grad_rows * grad_rows + grad_cols * grad_cols - weight * laplace / amp
    out_ref[...] = result[:, None, :]
    pltpu.make_async_copy(landed, landed, send_sem).wait()


def on_device(spectra, pick_bins, path_cells):
    per_count = lax.axis_size("per")
    sta_count = lax.axis_size("sta")
    per_place = lax.axis_index("per")
    count, _, band = spectra.shape
    pairs = count * count
    periods = pick_bins.shape[0]
    offs = pick_bins.shape[2] // count
    parts = jnp.transpose(spectra, (1, 0, 2))

    def along(value, by):
        return lax.ppermute(value, "sta", [(i, (i + by) % sta_count) for i in range(sta_count)])

    near = along(parts, 1)
    far = along(parts, 2)
    swap = [(0, 1), (1, 0)]
    bins_other = lax.ppermute(pick_bins, "per", swap)
    cells_other = lax.ppermute(path_cells, "per", swap)
    first = per_place == 0
    bins = jnp.concatenate(
        [jnp.where(first, pick_bins, bins_other), jnp.where(first, bins_other, pick_bins)], axis=1)
    cells = jnp.concatenate(
        [jnp.where(first, path_cells, cells_other), jnp.where(first, cells_other, path_cells)], axis=0)
    bins = jnp.transpose(bins.reshape(periods, count, offs, count), (0, 2, 1, 3)).reshape(periods, -1)
    cells = jnp.transpose(cells.reshape(count, 2, offs, count), (1, 2, 0, 3)).reshape(1, -1)

    coarse, fine = angle_tables(per_count)
    vmem = pl.BlockSpec(memory_space=pltpu.VMEM)
    table, corr = pl.pallas_call(
        own_kernel,
        out_shape=(jax.ShapeDtypeStruct((2, band, NLAG), jnp.bfloat16),
                   jax.ShapeDtypeStruct((pairs, NLAG), jnp.float32)),
        in_specs=[vmem] * 3,
        out_specs=(vmem, vmem),
        cost_estimate=pl.CostEstimate(flops=2 * pairs * 2 * band * NLAG, bytes_accessed=4 << 20, transcendentals=0),
        name="own_block",
    )(parts, coarse, fine)
    picks = pl.pallas_call(
        visit_kernel,
        out_shape=jax.ShapeDtypeStruct((per_count, periods // 2, offs * pairs), jnp.float32),
        in_specs=[vmem] * 6,
        out_specs=vmem,
        scratch_shapes=[pltpu.VMEM((pairs, NLAG), jnp.float32)] * 2,
        cost_estimate=pl.CostEstimate(flops=4 * pairs * 2 * band * NLAG, bytes_accessed=4 << 20, transcendentals=0),
        name="visiting_blocks",
    )(parts, near, far, table, corr, bins)
    rows = 2 * periods // per_count
    return pl.pallas_call(
        functools.partial(map_kernel, sta_count),
        out_shape=jax.ShapeDtypeStruct((periods // per_count, 1, 128), jnp.float32),
        in_specs=[vmem] * 2,
        out_specs=vmem,
        scratch_shapes=[
            pltpu.VMEM((periods // 2, offs * pairs), jnp.float32),
            pltpu.VMEM((sta_count, rows, 128), jnp.float32),
            pltpu.VMEM((sta_count - 1, rows, 128), jnp.float32),
            pltpu.VMEM((rows, 128), jnp.float32),
            pltpu.VMEM((2, rows, 128), jnp.float32),
            pltpu.VMEM((sta_count * 2 * rows, 2 * offs * pairs), jnp.bfloat16),
            pltpu.SemaphoreType.DMA((2,)),
            pltpu.SemaphoreType.DMA,
            pltpu.SemaphoreType.DMA,
            pltpu.SemaphoreType.DMA((2,)),
            pltpu.SemaphoreType.DMA((2,)),
        ],
        compiler_params=pltpu.CompilerParams(collective_id=0, has_side_effects=True),
        name="map_exchange",
    )(picks, cells)


def solution(mesh):
    return jax.shard_map(
        on_device,
        mesh=mesh,
        in_specs=(
            P("sta", None, "per"),
            P(None, ("sta", "per"), None),
            P(("sta", "per"), None, None),
        ),
        out_specs=P("per", "sta", None),
        check_vma=False,
    )
```

```python
import functools
import math

import jax
import jax.numpy as jnp
import numpy as np
from jax import lax
from jax.experimental import pallas as pl
from jax.experimental.pallas import tpu as pltpu
from jax.sharding import PartitionSpec as P

FREQ = 8192
NLAG = 128
COARSE = 128
CHUNK = 512
MESH = pl.DeviceIdType.MESH


def angle_tables(per_count):
    lag = np.arange(NLAG, dtype=np.int64) - NLAG // 2
    coarse = np.arange(FREQ // COARSE, dtype=np.int64) * COARSE
    fine = np.arange(COARSE, dtype=np.int64)
    out = []
    for bins, scale in ((coarse, FREQ ** -0.5), (fine, 1.0)):
        turned = (bins[:, None] * lag[None, :]) % (2 * FREQ)
        phase = turned.astype(np.float64) * (math.pi / FREQ)
        out.append(np.stack([np.cos(phase), np.sin(phase)]).astype(np.float32) * np.float32(scale))
    coarse_table, fine_table = out
    coarse_table = coarse_table.reshape(2, per_count, -1, NLAG).transpose(1, 0, 2, 3)
    return coarse_table, fine_table


def build_table(coarse_ref, fine_ref, table_ref, per_place):
    band = table_ref.shape[1]

    def one(step, carry):
        c = coarse_ref[per_place, 0, pl.ds(step, 1), :]
        s = coarse_ref[per_place, 1, pl.ds(step, 1), :]
        rows = pl.ds(pl.multiple_of(step * COARSE, COARSE), COARSE)
        fc = fine_ref[0]
        fs = fine_ref[1]
        table_ref[0, rows, :] = (c * fc - s * fs).astype(jnp.bfloat16)
        table_ref[1, rows, :] = (-(s * fc + c * fs)).astype(jnp.bfloat16)
        return carry

    lax.fori_loop(0, band // COARSE, one, 0)


def correlate_into(acc_refs, res_ref, vis_refs, table_ref, chunk):
    count = res_ref.shape[1]
    band = res_ref.shape[2]
    for acc in acc_refs:
        acc[...] = jnp.zeros_like(acc)

    def one(step, carry):
        cols = pl.ds(pl.multiple_of(step * chunk, chunk), chunk)
        cos_part = table_ref[0, cols, :]
        sin_part = table_ref[1, cols, :]
        rre = res_ref[0, :, cols].astype(jnp.float32)
        rim = res_ref[1, :, cols].astype(jnp.float32)
        for acc, vis in zip(acc_refs, vis_refs):
            vre = vis[0, :, cols].astype(jnp.float32)
            vim = vis[1, :, cols].astype(jnp.float32)
            res, ims = [], []
            for i in range(count):
                a = rre[i:i + 1]
                b = rim[i:i + 1]
                res.append((a * vre + b * vim).astype(jnp.bfloat16))
                ims.append((b * vre - a * vim).astype(jnp.bfloat16))
            cre = jnp.concatenate(res, axis=0)
            cim = jnp.concatenate(ims, axis=0)
            acc[...] += jnp.dot(cre, cos_part, preferred_element_type=jnp.float32) + jnp.dot(
                cim, sin_part, preferred_element_type=jnp.float32
            )
        return carry

    lax.fori_loop(0, band // chunk, one, 0)


def take_picks(acc, bins, is_own):
    turned = acc.T
    periods, pairs = bins.shape
    lag = lax.broadcasted_iota(jnp.int32, turned.shape, 0)
    rows = []
    for p in range(periods):
        rows.append(jnp.sum(jnp.where(lag == bins[p:p + 1], turned, 0.0), axis=0, keepdims=True))
    got = jnp.concatenate(rows, axis=0)
    if is_own:
        side = int(math.isqrt(pairs))
        place = lax.broadcasted_iota(jnp.int32, got.shape, 1)
        got = jnp.where(place // side == place % side, 0.0, got)
    return got


def kernel(sta_count, offs, parts_ref, bins_ref, cells_ref, coarse_ref, fine_ref, out_ref,
           near, far, all_bins, all_cells, table, accs, picks, peer_picks, spread, landed, edge_own, edges,
           lhs, block_send, block_recv, index_send, index_recv, pick_sems, send_sem, recv_sem, edge_send, edge_recv):
    sta = lax.axis_index("sta")
    per = lax.axis_index("per")
    count = parts_ref.shape[1]
    pairs = count * count
    barrier = pltpu.get_barrier_semaphore()
    pl.semaphore_signal(barrier, inc=1, device_id=(sta, 1 - per), device_id_type=MESH)

    def greet(step, carry):
        there = lax.rem(sta + step, sta_count)
        pl.semaphore_signal(barrier, inc=1, device_id=(there, per), device_id_type=MESH)
        return carry

    lax.fori_loop(1, sta_count, greet, 0)

    build_table(coarse_ref, fine_ref, table, per)
    correlate_into([accs.at[0]], parts_ref, [parts_ref], table, CHUNK)

    pl.semaphore_wait(barrier, sta_count)

    def sent(src, dst, send, recv, there, half):
        copy = pltpu.make_async_remote_copy(
            src_ref=src, dst_ref=dst, send_sem=send, recv_sem=recv, device_id=(there, half), device_id_type=MESH)
        copy.start()
        return copy

    near_copy = sent(parts_ref, near, block_send.at[0], block_recv.at[0], lax.rem(sta + 1, sta_count), per)
    bins_copy = sent(bins_ref, all_bins.at[per], index_send.at[0], index_recv.at[0], sta, 1 - per)
    cells_copy = sent(cells_ref, all_cells.at[per], index_send.at[1], index_recv.at[1], sta, 1 - per)
    far_copy = sent(parts_ref, far, block_send.at[1], block_recv.at[1], lax.rem(sta + 2, sta_count), per)
    all_bins[per] = bins_ref[...]
    all_cells[per] = cells_ref[...]
    bins_copy.wait()
    cells_copy.wait()

    halves, residents = all_bins.shape[0], all_bins.shape[2]
    bins, cells = [], []
    for k in range(offs):
        cols = slice(k * count, (k + 1) * count)
        where = [(h, i) for h in range(halves) for i in range(residents)]
        bins.append(jnp.concatenate([all_bins[h, :, i, cols] for h, i in where], axis=1))
        cells.append(jnp.concatenate([all_cells[h, i, :, cols] for h, i in where], axis=1))
    cell = jnp.concatenate(cells, axis=1)
    ends = cell.shape[1]
    col = cell % 128
    row = cell // 128
    row = jnp.concatenate([row[0:1], row[1:2]], axis=1)
    col = jnp.concatenate([col[0:1], col[1:2]], axis=1)
    col_hot = (lax.broadcasted_iota(jnp.int32, (128, 2 * ends), 0) == col).astype(jnp.bfloat16)

    half = picks.shape[1]

    def pick(k):
        got = take_picks(accs[k], bins[k], k == 0)
        picks[0, :, k * pairs:(k + 1) * pairs] = got[:half]
        picks[1, :, k * pairs:(k + 1) * pairs] = got[half:]

    pick(0)
    near_copy.wait()
    correlate_into([accs.at[1]], parts_ref, [near], table, CHUNK)
    pick(1)
    far_copy.wait()
    correlate_into([accs.at[2]], parts_ref, [far], table, CHUNK)
    pick(2)

    trade = sent(picks.at[1 - per], peer_picks, pick_sems.at[0], pick_sems.at[1], sta, 1 - per)
    trade.wait()
    total = picks[per] + peer_picks[...]
    both = jnp.concatenate([total, total * total], axis=0)
    rows = both.shape[0]
    high = both.astype(jnp.bfloat16).astype(jnp.float32)
    low = both - high
    vals = jnp.concatenate([high, low], axis=0)
    vals = jnp.concatenate([vals, vals], axis=1)
    row = jnp.broadcast_to(row, vals.shape)

    group = 16
    for first in range(0, sta_count, group):
        for r in range(group):
            wanted = lax.rem(sta + (first + r), sta_count)
            lhs[r * 2 * rows:(r + 1) * 2 * rows, :] = jnp.where(row == wanted, vals, 0.0).astype(jnp.bfloat16)
        grid = lax.dot_general(lhs[...], col_hot, (((1,), (1,)), ((), ())), preferred_element_type=jnp.float32)
        grid = grid.reshape(group, 2, rows, 128)
        spread[first:first + group] = grid[:, 0] + grid[:, 1]

        def send(step, carry):
            sent(spread.at[step], landed.at[step - 1], send_sem, recv_sem, lax.rem(sta + step, sta_count), per)
            return carry

        lax.fori_loop(max(first, 1), first + group, send, 0)

    pltpu.make_async_copy(landed, landed, recv_sem).wait()
    edge_own[...] = spread[0] + jnp.sum(landed[...], axis=0)
    copies = [sent(edge_own, edges.at[side], edge_send.at[side], edge_recv.at[side], lax.rem(sta + step, sta_count), per)
              for side, step in enumerate((1, sta_count - 1))]
    own = edge_own[...]
    half = own.shape[0] // 2
    lane = lax.broadcasted_iota(jnp.int32, own.shape, 1)
    before_col = jnp.where(lane == 0, 0.0, pltpu.roll(own, 1, 1))
    after_col = jnp.where(lane == 127, 0.0, pltpu.roll(own, 127, 1))
    for copy in copies:
        copy.wait()
    before = jnp.where(sta == 0, 0.0, edges[0])
    after = jnp.where(sta == sta_count - 1, 0.0, edges[1])
    grad_rows = (after[:half] - before[:half]) * 0.5
    grad_cols = (after_col[:half] - before_col[:half]) * 0.5
    amp = 1.0 + own[half:]
    laplace = ((1.0 + after[half:]) + (1.0 + before[half:]) + (1.0 + after_col[half:])
               + (1.0 + before_col[half:]) - 4.0 * amp)
    period = per * half + lax.broadcasted_iota(jnp.int32, laplace.shape, 0)
    weight = 1.0 / (1.0 + period.astype(jnp.float32))
    result = grad_rows * grad_rows + grad_cols * grad_cols - weight * laplace / amp
    out_ref[...] = result[:, None, :]
    pltpu.make_async_copy(landed, landed, send_sem).wait()


def on_device(spectra, pick_bins, path_cells):
    per_count = lax.axis_size("per")
    sta_count = lax.axis_size("sta")
    count, _, band = spectra.shape
    pairs = count * count
    periods = pick_bins.shape[0]
    offs = pick_bins.shape[2] // count
    parts = jnp.transpose(spectra, (1, 0, 2))
    coarse, fine = angle_tables(per_count)
    local = periods // per_count
    rows = 2 * local
    vmem = pl.BlockSpec(memory_space=pltpu.VMEM)
    dma = pltpu.SemaphoreType.DMA
    return pl.pallas_call(
        functools.partial(kernel, sta_count, offs),
        out_shape=jax.ShapeDtypeStruct((local, 1, 128), jnp.float32),
        in_specs=[vmem] * 5,
        out_specs=vmem,
        scratch_shapes=[
            pltpu.VMEM(parts.shape, parts.dtype),
            pltpu.VMEM(parts.shape, parts.dtype),
            pltpu.VMEM((per_count,) + pick_bins.shape, jnp.int32),
            pltpu.VMEM((per_count,) + path_cells.shape, jnp.int32),
            pltpu.VMEM((2, band, NLAG), jnp.bfloat16),
            pltpu.VMEM((offs, pairs, NLAG), jnp.float32),
            pltpu.VMEM((per_count, local, offs * pairs), jnp.float32),
            pltpu.VMEM((local, offs * pairs), jnp.float32),
            pltpu.VMEM((sta_count, rows, 128), jnp.float32),
            pltpu.VMEM((sta_count - 1, rows, 128), jnp.float32),
            pltpu.VMEM((rows, 128), jnp.float32),
            pltpu.VMEM((2, rows, 128), jnp.float32),
            pltpu.VMEM((16 * 2 * rows, 2 * offs * pairs), jnp.bfloat16),
            dma((2,)), dma((2,)), dma((2,)), dma((2,)), dma((2,)), dma, dma, dma((2,)), dma((2,)),
        ],
        compiler_params=pltpu.CompilerParams(collective_id=0, has_side_effects=True),
        name="noise_map",
    )(parts, pick_bins, path_cells, coarse, fine)


def solution(mesh):
    return jax.shard_map(
        on_device,
        mesh=mesh,
        in_specs=(
            P("sta", None, "per"),
            P(None, ("sta", "per"), None),
            P(("sta", "per"), None, None),
        ),
        out_specs=P("per", "sta", None),
        check_vma=False,
    )
```

```python
import functools
import math

import jax
import jax.numpy as jnp
import numpy as np
from jax import lax
from jax.experimental import pallas as pl
from jax.experimental.pallas import tpu as pltpu
from jax.sharding import PartitionSpec as P

FREQ = 8192
NLAG = 128
COARSE = 128
CHUNK = 512
PIECES = 2
GROUP = 16
MESH = pl.DeviceIdType.MESH


def angle_tables(per_count):
    lag = np.arange(NLAG, dtype=np.int64) - NLAG // 2
    coarse = np.arange(FREQ // COARSE, dtype=np.int64) * COARSE
    fine = np.arange(COARSE, dtype=np.int64)
    out = []
    for bins, scale in ((coarse, FREQ ** -0.5), (fine, 1.0)):
        turned = (bins[:, None] * lag[None, :]) % (2 * FREQ)
        phase = turned.astype(np.float64) * (math.pi / FREQ)
        out.append(np.stack([np.cos(phase), np.sin(phase)]).astype(np.float32) * np.float32(scale))
    coarse_table, fine_table = out
    coarse_table = coarse_table.reshape(2, per_count, -1, NLAG).transpose(1, 0, 2, 3)
    return coarse_table, fine_table


def build_table(coarse_ref, fine_ref, table_ref, per_place):
    band = table_ref.shape[1]

    def one(step, carry):
        c = coarse_ref[per_place, 0, pl.ds(step, 1), :]
        s = coarse_ref[per_place, 1, pl.ds(step, 1), :]
        rows = pl.ds(pl.multiple_of(step * COARSE, COARSE), COARSE)
        fc = fine_ref[0]
        fs = fine_ref[1]
        table_ref[0, rows, :] = (c * fc - s * fs).astype(jnp.bfloat16)
        table_ref[1, rows, :] = (-(s * fc + c * fs)).astype(jnp.bfloat16)
        return carry

    lax.fori_loop(0, band // COARSE, one, 0)


def correlate_into(acc, resident, visiting, table_ref, start, stop):
    count = resident.shape[1]
    if start == 0:
        acc[...] = jnp.zeros_like(acc)

    def one(step, carry):
        cols = pl.ds(pl.multiple_of(step * CHUNK, CHUNK), CHUNK)
        rre = resident[0, :, cols].astype(jnp.float32)
        rim = resident[1, :, cols].astype(jnp.float32)
        vre = visiting[0, :, cols].astype(jnp.float32)
        vim = visiting[1, :, cols].astype(jnp.float32)
        real, imag = [], []
        for i in range(count):
            a = rre[i:i + 1]
            b = rim[i:i + 1]
            real.append((a * vre + b * vim).astype(jnp.bfloat16))
            imag.append((b * vre - a * vim).astype(jnp.bfloat16))
        real = jnp.concatenate(real, axis=0)
        imag = jnp.concatenate(imag, axis=0)
        acc[...] += jnp.dot(real, table_ref[0, cols, :], preferred_element_type=jnp.float32) + jnp.dot(
            imag, table_ref[1, cols, :], preferred_element_type=jnp.float32
        )
        return carry

    lax.fori_loop(start // CHUNK, stop // CHUNK, one, 0)


def take_picks(acc, bins, is_own):
    turned = acc.T
    periods, pairs = bins.shape
    lag = lax.broadcasted_iota(jnp.int32, turned.shape, 0)
    rows = []
    for p in range(periods):
        rows.append(jnp.sum(jnp.where(lag == bins[p:p + 1], turned, 0.0), axis=0, keepdims=True))
    got = jnp.concatenate(rows, axis=0)
    if is_own:
        side = int(math.isqrt(pairs))
        place = lax.broadcasted_iota(jnp.int32, got.shape, 1)
        got = jnp.where(place // side == place % side, 0.0, got)
    return got


def kernel(sta_count, offs, parts_ref, bins_ref, cells_ref, coarse_ref, fine_ref, out_ref,
           blocks, all_bins, all_cells, table, accs, picks, peer_picks, spread, landed, edge_own, edges, lhs_first, lhs,
           own_sem, near_send, near_recv, far_send, far_recv, index_send, index_recv, row_sem, col_sem,
           pick_send, pick_recv, send_sem, recv_sem, edge_send, edge_recv):
    sta = lax.axis_index("sta")
    per = lax.axis_index("per")
    even = lax.rem(sta, 2) == 0
    count = blocks.shape[2]
    band = blocks.shape[3]
    pairs = count * count
    piece = band // PIECES

    def around(step):
        return lax.rem(sta + (step + sta_count), sta_count)

    def digit_peers(stride):
        place = lax.rem(sta // stride, 4)
        return [sta + stride * (lax.rem(place + step, 4) - place) for step in (1, 2, 3)]

    def signal(sem, there, half):
        pl.semaphore_signal(sem, inc=1, device_id=(there, half), device_id_type=MESH)

    barrier = pltpu.get_barrier_semaphore()
    signal(barrier, sta, 1 - per)
    for step in (1, -1, 2, -2):
        signal(barrier, around(step), per)
    for step in (2, -2):
        signal(barrier, around(step), 1 - per)
    for stride in (1, 4, 16):
        for there in digit_peers(stride):
            signal(barrier, there, per)

    own = pltpu.make_async_copy(parts_ref, blocks.at[0], own_sem)
    own.start()
    build_table(coarse_ref, fine_ref, table, per)
    own.wait()
    pl.semaphore_wait(barrier, 16)

    def copy(src, dst, send, recv, there, half):
        return pltpu.make_async_remote_copy(
            src_ref=src, dst_ref=dst, send_sem=send, recv_sem=recv, device_id=(there, half), device_id_type=MESH)

    def index_copies(there, half, slot, sems):
        return [copy(bins_ref, all_bins.at[slot, per], index_send.at[sems, 0], index_recv.at[slot, per, 0], there, half),
                copy(cells_ref, all_cells.at[slot, per], index_send.at[sems, 1], index_recv.at[slot, per, 1], there, half)]

    def cut(slot, number):
        return blocks.at[slot, :, :, pl.ds(number * piece, piece)]

    for c in index_copies(sta, 1 - per, 0, 0):
        c.start()
    near = [copy(cut(0, n), cut(1, n), near_send.at[n], near_recv.at[n], around(1), per) for n in range(PIECES)]
    back = [copy(cut(0, n), cut(2, n), far_send.at[0, n], far_recv.at[n], around(-2), per) for n in range(PIECES)]
    along = [copy(cut(1, n), cut(2, n), far_send.at[1, n], far_recv.at[n], around(1), per) for n in range(PIECES)]
    for n in range(PIECES):
        near[n].start()

        @pl.when(even)
        def _():
            back[n].start()

    @pl.when(even)
    def _():
        for half, sems in ((per, 1), (1 - per, 2)):
            for c in index_copies(around(-2), half, 1, sems):
                c.start()

    for there in digit_peers(16):
        signal(row_sem, there, per)

    correlate_into(accs.at[0], blocks.at[0], blocks.at[0], table, 0, band)

    pl.semaphore_wait(row_sem, 3)
    for there in digit_peers(4):
        signal(col_sem, there, per)

    all_bins[0, per] = bins_ref[...]
    all_cells[0, per] = cells_ref[...]
    for ref, kind in ((bins_ref, 0), (cells_ref, 1)):
        pltpu.make_async_copy(ref, ref, index_recv.at[0, 1 - per, kind]).wait()
        pltpu.make_async_copy(ref, ref, index_send.at[0, kind]).wait()

    @pl.when(even)
    def _():
        for half in range(2):
            for ref, kind in ((bins_ref, 0), (cells_ref, 1)):
                pltpu.make_async_copy(ref, ref, index_recv.at[1, half, kind]).wait()
                pltpu.make_async_copy(ref, ref, index_send.at[1 + half, kind]).wait()

    far_set = jnp.where(even, 1, 0)
    halves, residents = all_bins.shape[1], all_bins.shape[3]
    spots = [(h, i) for h in range(halves) for i in range(residents)]

    def bins_of(k):
        cols = slice(k * count, (k + 1) * count)
        which = far_set if k == offs - 1 else 0
        return jnp.concatenate([all_bins[which, h, :, i, cols] for h, i in spots], axis=1)

    def cells_of(k):
        cols = slice(k * count, (k + 1) * count)
        which = far_set if k == offs - 1 else 0
        return jnp.concatenate([all_cells[which, h, i, :, cols] for h, i in spots], axis=1)

    half = picks.shape[1]

    def pick(k):
        got = take_picks(accs[k], bins_of(k), k == 0)
        picks[0, :, k * pairs:(k + 1) * pairs] = got[:half]
        picks[1, :, k * pairs:(k + 1) * pairs] = got[half:]

    pick(0)
    for n in range(PIECES):
        near[n].wait_recv()

        @pl.when(even)
        def _():
            along[n].start()

        correlate_into(accs.at[1], blocks.at[0], blocks.at[1], table, n * piece, (n + 1) * piece)
    pick(1)

    def trade(number, start, stop):
        lanes = pl.ds(start, stop - start)
        return copy(picks.at[1 - per, :, lanes], peer_picks.at[:, lanes], pick_send.at[number], pick_recv.at[number],
                    sta, 1 - per)

    split = (offs - 1) * pairs
    first_trade = trade(0, 0, split)
    first_trade.start()
    resident = blocks.at[jnp.where(even, 2, 0)]
    visiting = blocks.at[jnp.where(even, 0, 2)]
    for n in range(PIECES):
        back[n].wait_recv()
        correlate_into(accs.at[2], resident, visiting, table, n * piece, (n + 1) * piece)
    pick(2)
    last_trade = trade(1, split, offs * pairs)
    last_trade.start()
    pl.semaphore_wait(col_sem, 3)

    rows = 2 * half

    def ends_of(ks):
        cell = jnp.concatenate([cells_of(k) for k in ks], axis=1)
        row = cell // 128
        col = cell % 128
        row = jnp.concatenate([row[0:1], row[1:2]], axis=1)
        col = jnp.concatenate([col[0:1], col[1:2]], axis=1)
        hot = (lax.broadcasted_iota(jnp.int32, (128, col.shape[1]), 0) == col).astype(jnp.bfloat16)
        return jnp.broadcast_to(row, (2 * rows, row.shape[1])), hot

    def values(start, stop):
        total = picks[per, :, start:stop] + peer_picks[:, start:stop]
        both = jnp.concatenate([total, total * total], axis=0)
        high = both.astype(jnp.bfloat16).astype(jnp.float32)
        vals = jnp.concatenate([high, both - high], axis=0)
        return jnp.concatenate([vals, vals], axis=1)

    def add_up(lhs_ref, first, group, row, vals, hot):
        for r in range(group):
            wanted = around(first + r)
            lhs_ref[r * 2 * rows:(r + 1) * 2 * rows, :] = jnp.where(row == wanted, vals, 0.0).astype(jnp.bfloat16)
        grid = lax.dot_general(lhs_ref[...], hot, (((1,), (1,)), ((), ())), preferred_element_type=jnp.float32)
        grid = grid.reshape(group, 2, rows, 128)
        return grid[:, 0] + grid[:, 1]

    row, hot = ends_of(range(offs - 1))
    first_trade.wait()
    vals = values(0, split)
    for first in range(0, sta_count, GROUP):
        spread[first:first + GROUP] = add_up(lhs_first, first, GROUP, row, vals, hot)
    row, hot = ends_of([offs - 1])
    last_trade.wait()
    vals = values(split, offs * pairs)
    for first in range(0, sta_count, GROUP):
        spread[first:first + GROUP] += add_up(lhs, first, GROUP, row, vals, hot)

        def send(step, carry):
            copy(spread.at[step], landed.at[step - 1], send_sem, recv_sem, around(step), per).start()
            return carry

        lax.fori_loop(max(first, 1), first + GROUP, send, 0)

    for n in range(PIECES):
        near[n].wait_send()

        @pl.when(even)
        def _():
            back[n].wait_send()
            along[n].wait_send()

    pltpu.make_async_copy(landed, landed, recv_sem).wait()
    edge_own[...] = spread[0] + jnp.sum(landed[...], axis=0)
    sides = [copy(edge_own, edges.at[side], edge_send.at[side], edge_recv.at[side], around(step), per)
             for side, step in enumerate((1, -1))]
    for c in sides:
        c.start()
    mine = edge_own[...]
    lane = lax.broadcasted_iota(jnp.int32, mine.shape, 1)
    before_col = jnp.where(lane == 0, 0.0, pltpu.roll(mine, 1, 1))
    after_col = jnp.where(lane == 127, 0.0, pltpu.roll(mine, 127, 1))
    for c in sides:
        c.wait()
    before = jnp.where(sta == 0, 0.0, edges[0])
    after = jnp.where(sta == sta_count - 1, 0.0, edges[1])
    grad_rows = (after[:half] - before[:half]) * 0.5
    grad_cols = (after_col[:half] - before_col[:half]) * 0.5
    amp = 1.0 + mine[half:]
    laplace = ((1.0 + after[half:]) + (1.0 + before[half:]) + (1.0 + after_col[half:])
               + (1.0 + before_col[half:]) - 4.0 * amp)
    period = per * half + lax.broadcasted_iota(jnp.int32, laplace.shape, 0)
    weight = 1.0 / (1.0 + period.astype(jnp.float32))
    result = grad_rows * grad_rows + grad_cols * grad_cols - weight * laplace / amp
    out_ref[...] = result[:, None, :]
    pltpu.make_async_copy(landed, landed, send_sem).wait()


def on_device(spectra, pick_bins, path_cells):
    per_count = lax.axis_size("per")
    sta_count = lax.axis_size("sta")
    count, _, band = spectra.shape
    pairs = count * count
    periods = pick_bins.shape[0]
    offs = pick_bins.shape[2] // count
    parts = jnp.transpose(spectra, (1, 0, 2))
    coarse, fine = angle_tables(per_count)
    local = periods // per_count
    rows = 2 * local
    vmem = pl.BlockSpec(memory_space=pltpu.VMEM)
    dma = pltpu.SemaphoreType.DMA
    regular = pltpu.SemaphoreType.REGULAR
    return pl.pallas_call(
        functools.partial(kernel, sta_count, offs),
        out_shape=jax.ShapeDtypeStruct((local, 1, 128), jnp.float32),
        in_specs=[pl.BlockSpec(memory_space=pl.ANY)] + [vmem] * 4,
        out_specs=vmem,
        scratch_shapes=[
            pltpu.VMEM((3,) + parts.shape, parts.dtype),
            pltpu.VMEM((2, per_count) + pick_bins.shape, jnp.int32),
            pltpu.VMEM((2, per_count) + path_cells.shape, jnp.int32),
            pltpu.VMEM((2, band, NLAG), jnp.bfloat16),
            pltpu.VMEM((offs, pairs, NLAG), jnp.float32),
            pltpu.VMEM((per_count, local, offs * pairs), jnp.float32),
            pltpu.VMEM((local, offs * pairs), jnp.float32),
            pltpu.VMEM((sta_count, rows, 128), jnp.float32),
            pltpu.VMEM((sta_count - 1, rows, 128), jnp.float32),
            pltpu.VMEM((rows, 128), jnp.float32),
            pltpu.VMEM((2, rows, 128), jnp.float32),
            pltpu.VMEM((GROUP * 2 * rows, 2 * (offs - 1) * pairs), jnp.bfloat16),
            pltpu.VMEM((GROUP * 2 * rows, 2 * pairs), jnp.bfloat16),
            dma, dma((PIECES,)), dma((PIECES,)), dma((2, PIECES)), dma((PIECES,)), dma((3, 2)), dma((2, 2, 2)),
            regular, regular, dma((2,)), dma((2,)), dma, dma, dma((2,)), dma((2,)),
        ],
        compiler_params=pltpu.CompilerParams(collective_id=0, has_side_effects=True),
        name="noise_map",
    )(parts, pick_bins, path_cells, coarse, fine)


def solution(mesh):
    return jax.shard_map(
        on_device,
        mesh=mesh,
        in_specs=(
            P("sta", None, "per"),
            P(None, ("sta", "per"), None),
            P(("sta", "per"), None, None),
        ),
        out_specs=P("per", "sta", None),
        check_vma=False,
    )
```

```python
import functools
import math

import jax
import jax.numpy as jnp
import numpy as np
from jax import lax
from jax.experimental import pallas as pl
from jax.experimental.pallas import tpu as pltpu
from jax.sharding import PartitionSpec as P

FREQ = 8192
NLAG = 128
COARSE = 128
CHUNK = 512
PIECES = 2
GROUP = 16
MESH = pl.DeviceIdType.MESH


def angle_tables(per_count):
    lag = np.arange(NLAG, dtype=np.int64) - NLAG // 2
    coarse = np.arange(FREQ // COARSE, dtype=np.int64) * COARSE
    fine = np.arange(COARSE, dtype=np.int64)
    out = []
    for bins, scale in ((coarse, FREQ ** -0.5), (fine, 1.0)):
        turned = (bins[:, None] * lag[None, :]) % (2 * FREQ)
        phase = turned.astype(np.float64) * (math.pi / FREQ)
        out.append(np.stack([np.cos(phase), np.sin(phase)]).astype(np.float32) * np.float32(scale))
    coarse_table, fine_table = out
    coarse_table = coarse_table.reshape(2, per_count, -1, NLAG).transpose(1, 0, 2, 3)
    return coarse_table, fine_table


def build_table(coarse_ref, fine_ref, table_ref, per_place):
    band = table_ref.shape[1]

    def one(step, carry):
        c = coarse_ref[per_place, 0, pl.ds(step, 1), :]
        s = coarse_ref[per_place, 1, pl.ds(step, 1), :]
        rows = pl.ds(pl.multiple_of(step * COARSE, COARSE), COARSE)
        fc = fine_ref[0]
        fs = fine_ref[1]
        table_ref[0, rows, :] = (c * fc - s * fs).astype(jnp.bfloat16)
        table_ref[1, rows, :] = (-(s * fc + c * fs)).astype(jnp.bfloat16)
        return carry

    lax.fori_loop(0, band // COARSE, one, 0)


def correlate_into(acc, resident, visiting, table_ref, start, stop):
    count = resident.shape[1]
    if start == 0:
        acc[...] = jnp.zeros_like(acc)

    def one(step, carry):
        cols = pl.ds(pl.multiple_of(step * CHUNK, CHUNK), CHUNK)
        rre = resident[0, :, cols].astype(jnp.float32)
        rim = resident[1, :, cols].astype(jnp.float32)
        vre = visiting[0, :, cols].astype(jnp.float32)
        vim = visiting[1, :, cols].astype(jnp.float32)
        real, imag = [], []
        for i in range(count):
            a = rre[i:i + 1]
            b = rim[i:i + 1]
            real.append((a * vre + b * vim).astype(jnp.bfloat16))
            imag.append((b * vre - a * vim).astype(jnp.bfloat16))
        real = jnp.concatenate(real, axis=0)
        imag = jnp.concatenate(imag, axis=0)
        acc[...] += jnp.dot(real, table_ref[0, cols, :], preferred_element_type=jnp.float32) + jnp.dot(
            imag, table_ref[1, cols, :], preferred_element_type=jnp.float32
        )
        return carry

    lax.fori_loop(start // CHUNK, stop // CHUNK, one, 0)


def take_picks(acc, bins, is_own):
    turned = acc.T
    periods, pairs = bins.shape
    lag = lax.broadcasted_iota(jnp.int32, turned.shape, 0)
    rows = []
    for p in range(periods):
        rows.append(jnp.sum(jnp.where(lag == bins[p:p + 1], turned, 0.0), axis=0, keepdims=True))
    got = jnp.concatenate(rows, axis=0)
    if is_own:
        side = int(math.isqrt(pairs))
        place = lax.broadcasted_iota(jnp.int32, got.shape, 1)
        got = jnp.where(place // side == place % side, 0.0, got)
    return got


def kernel(sta_count, offs, parts_ref, bins_ref, cells_ref, coarse_ref, fine_ref, out_ref,
           blocks, all_bins, all_cells, table, accs, picks, peer_picks, spread, landed, edge_own, edges, lhs_first, lhs,
           own_sem, near_send, near_recv, far_send, far_recv, index_send, index_recv, row_sem, col_sem,
           pick_send, pick_recv, send_sem, recv_sem, edge_send, edge_recv):
    sta = lax.axis_index("sta")
    per = lax.axis_index("per")
    even = lax.rem(sta, 2) == 0
    count = blocks.shape[2]
    band = blocks.shape[3]
    pairs = count * count
    piece = band // PIECES

    def around(step):
        return lax.rem(sta + (step + sta_count), sta_count)

    def digit_peers(stride):
        place = lax.rem(sta // stride, 4)
        return [sta + stride * (lax.rem(place + step, 4) - place) for step in (1, 2, 3)]

    def signal(sem, there, half):
        pl.semaphore_signal(sem, inc=1, device_id=(there, half), device_id_type=MESH)

    barrier = pltpu.get_barrier_semaphore()
    signal(barrier, sta, 1 - per)
    for step in (1, -1, 2, -2):
        signal(barrier, around(step), per)
    for step in (2, -2):
        signal(barrier, around(step), 1 - per)
    for stride in (1, 4, 16):
        for there in digit_peers(stride):
            signal(barrier, there, per)

    own = pltpu.make_async_copy(parts_ref, blocks.at[0], own_sem)
    own.start()
    own.wait()
    pl.semaphore_wait(barrier, 16)

    def copy(src, dst, send, recv, there, half):
        return pltpu.make_async_remote_copy(
            src_ref=src, dst_ref=dst, send_sem=send, recv_sem=recv, device_id=(there, half), device_id_type=MESH)

    def index_copies(there, half, slot, sems):
        return [copy(bins_ref, all_bins.at[slot, per], index_send.at[sems, 0], index_recv.at[slot, per, 0], there, half),
                copy(cells_ref, all_cells.at[slot, per], index_send.at[sems, 1], index_recv.at[slot, per, 1], there, half)]

    def cut(slot, number):
        return blocks.at[slot, :, :, pl.ds(number * piece, piece)]

    for c in index_copies(sta, 1 - per, 0, 0):
        c.start()
    near = [copy(cut(0, n), cut(1, n), near_send.at[n], near_recv.at[n], around(1), per) for n in range(PIECES)]
    back = [copy(cut(0, n), cut(2, n), far_send.at[0, n], far_recv.at[n], around(-2), per) for n in range(PIECES)]
    along = [copy(cut(1, n), cut(2, n), far_send.at[1, n], far_recv.at[n], around(1), per) for n in range(PIECES)]
    for n in range(PIECES):
        near[n].start()

        @pl.when(even)
        def _():
            back[n].start()

    @pl.when(even)
    def _():
        for half, sems in ((per, 1), (1 - per, 2)):
            for c in index_copies(around(-2), half, 1, sems):
                c.start()

    for there in digit_peers(16):
        signal(row_sem, there, per)

    build_table(coarse_ref, fine_ref, table, per)
    correlate_into(accs.at[0], blocks.at[0], blocks.at[0], table, 0, band)

    pl.semaphore_wait(row_sem, 3)
    for there in digit_peers(4):
        signal(col_sem, there, per)

    all_bins[0, per] = bins_ref[...]
    all_cells[0, per] = cells_ref[...]
    for ref, kind in ((bins_ref, 0), (cells_ref, 1)):
        pltpu.make_async_copy(ref, ref, index_recv.at[0, 1 - per, kind]).wait()
        pltpu.make_async_copy(ref, ref, index_send.at[0, kind]).wait()

    far_set = jnp.where(even, 1, 0)
    halves, residents = all_bins.shape[1], all_bins.shape[3]
    spots = [(h, i) for h in range(halves) for i in range(residents)]

    def bins_of(k):
        cols = slice(k * count, (k + 1) * count)
        which = far_set if k == offs - 1 else 0
        return jnp.concatenate([all_bins[which, h, :, i, cols] for h, i in spots], axis=1)

    def cells_of(k):
        cols = slice(k * count, (k + 1) * count)
        which = far_set if k == offs - 1 else 0
        return jnp.concatenate([all_cells[which, h, i, :, cols] for h, i in spots], axis=1)

    half = picks.shape[1]

    def pick(k):
        got = take_picks(accs[k], bins_of(k), k == 0)
        picks[0, :, k * pairs:(k + 1) * pairs] = got[:half]
        picks[1, :, k * pairs:(k + 1) * pairs] = got[half:]

    pick(0)
    for n in range(PIECES):
        near[n].wait_recv()

        @pl.when(even)
        def _():
            along[n].start()

        correlate_into(accs.at[1], blocks.at[0], blocks.at[1], table, n * piece, (n + 1) * piece)
    pick(1)

    def trade(number, start, stop):
        lanes = pl.ds(start, stop - start)
        return copy(picks.at[1 - per, :, lanes], peer_picks.at[:, lanes], pick_send.at[number], pick_recv.at[number],
                    sta, 1 - per)

    split = (offs - 1) * pairs
    first_trade = trade(0, 0, split)
    first_trade.start()
    resident = blocks.at[jnp.where(even, 2, 0)]
    visiting = blocks.at[jnp.where(even, 0, 2)]
    for n in range(PIECES):
        back[n].wait_recv()
        correlate_into(accs.at[2], resident, visiting, table, n * piece, (n + 1) * piece)

    @pl.when(even)
    def _():
        for half in range(2):
            for ref, kind in ((bins_ref, 0), (cells_ref, 1)):
                pltpu.make_async_copy(ref, ref, index_recv.at[1, half, kind]).wait()
                pltpu.make_async_copy(ref, ref, index_send.at[1 + half, kind]).wait()

    pick(2)
    last_trade = trade(1, split, offs * pairs)
    last_trade.start()
    pl.semaphore_wait(col_sem, 3)

    rows = 2 * half

    def ends_of(ks):
        cell = jnp.concatenate([cells_of(k) for k in ks], axis=1)
        row = cell // 128
        col = cell % 128
        row = jnp.concatenate([row[0:1], row[1:2]], axis=1)
        col = jnp.concatenate([col[0:1], col[1:2]], axis=1)
        hot = (lax.broadcasted_iota(jnp.int32, (128, col.shape[1]), 0) == col).astype(jnp.bfloat16)
        return jnp.broadcast_to(row, (2 * rows, row.shape[1])), hot

    def values(start, stop):
        total = picks[per, :, start:stop] + peer_picks[:, start:stop]
        both = jnp.concatenate([total, total * total], axis=0)
        high = both.astype(jnp.bfloat16).astype(jnp.float32)
        vals = jnp.concatenate([high, both - high], axis=0)
        return jnp.concatenate([vals, vals], axis=1)

    def add_up(lhs_ref, first, group, row, vals, hot):
        for r in range(group):
            wanted = around(first + r)
            lhs_ref[r * 2 * rows:(r + 1) * 2 * rows, :] = jnp.where(row == wanted, vals, 0.0).astype(jnp.bfloat16)
        grid = lax.dot_general(lhs_ref[...], hot, (((1,), (1,)), ((), ())), preferred_element_type=jnp.float32)
        grid = grid.reshape(group, 2, rows, 128)
        return grid[:, 0] + grid[:, 1]

    row, hot = ends_of(range(offs - 1))
    first_trade.wait()
    vals = values(0, split)
    for first in range(0, sta_count, GROUP):
        spread[first:first + GROUP] = add_up(lhs_first, first, GROUP, row, vals, hot)
    row, hot = ends_of([offs - 1])
    last_trade.wait()
    vals = values(split, offs * pairs)
    for first in range(0, sta_count, GROUP):
        spread[first:first + GROUP] += add_up(lhs, first, GROUP, row, vals, hot)

        def send(step, carry):
            copy(spread.at[step], landed.at[step - 1], send_sem, recv_sem, around(step), per).start()
            return carry

        lax.fori_loop(max(first, 1), first + GROUP, send, 0)

    for n in range(PIECES):
        near[n].wait_send()

        @pl.when(even)
        def _():
            back[n].wait_send()
            along[n].wait_send()

    pltpu.make_async_copy(landed, landed, recv_sem).wait()
    edge_own[...] = spread[0] + jnp.sum(landed[...], axis=0)
    sides = [copy(edge_own, edges.at[side], edge_send.at[side], edge_recv.at[side], around(step), per)
             for side, step in enumerate((1, -1))]
    for c in sides:
        c.start()
    mine = edge_own[...]
    lane = lax.broadcasted_iota(jnp.int32, mine.shape, 1)
    before_col = jnp.where(lane == 0, 0.0, pltpu.roll(mine, 1, 1))
    after_col = jnp.where(lane == 127, 0.0, pltpu.roll(mine, 127, 1))
    for c in sides:
        c.wait()
    before = jnp.where(sta == 0, 0.0, edges[0])
    after = jnp.where(sta == sta_count - 1, 0.0, edges[1])
    grad_rows = (after[:half] - before[:half]) * 0.5
    grad_cols = (after_col[:half] - before_col[:half]) * 0.5
    amp = 1.0 + mine[half:]
    laplace = ((1.0 + after[half:]) + (1.0 + before[half:]) + (1.0 + after_col[half:])
               + (1.0 + before_col[half:]) - 4.0 * amp)
    period = per * half + lax.broadcasted_iota(jnp.int32, laplace.shape, 0)
    weight = 1.0 / (1.0 + period.astype(jnp.float32))
    result = grad_rows * grad_rows + grad_cols * grad_cols - weight * laplace / amp
    out_ref[...] = result[:, None, :]
    pltpu.make_async_copy(landed, landed, send_sem).wait()


def on_device(spectra, pick_bins, path_cells):
    per_count = lax.axis_size("per")
    sta_count = lax.axis_size("sta")
    count, _, band = spectra.shape
    pairs = count * count
    periods = pick_bins.shape[0]
    offs = pick_bins.shape[2] // count
    parts = jnp.transpose(spectra, (1, 0, 2))
    coarse, fine = angle_tables(per_count)
    local = periods // per_count
    rows = 2 * local
    vmem = pl.BlockSpec(memory_space=pltpu.VMEM)
    dma = pltpu.SemaphoreType.DMA
    regular = pltpu.SemaphoreType.REGULAR
    return pl.pallas_call(
        functools.partial(kernel, sta_count, offs),
        out_shape=jax.ShapeDtypeStruct((local, 1, 128), jnp.float32),
        in_specs=[pl.BlockSpec(memory_space=pl.ANY)] + [vmem] * 4,
        out_specs=vmem,
        scratch_shapes=[
            pltpu.VMEM((3,) + parts.shape, parts.dtype),
            pltpu.VMEM((2, per_count) + pick_bins.shape, jnp.int32),
            pltpu.VMEM((2, per_count) + path_cells.shape, jnp.int32),
            pltpu.VMEM((2, band, NLAG), jnp.bfloat16),
            pltpu.VMEM((offs, pairs, NLAG), jnp.float32),
            pltpu.VMEM((per_count, local, offs * pairs), jnp.float32),
            pltpu.VMEM((local, offs * pairs), jnp.float32),
            pltpu.VMEM((sta_count, rows, 128), jnp.float32),
            pltpu.VMEM((sta_count - 1, rows, 128), jnp.float32),
            pltpu.VMEM((rows, 128), jnp.float32),
            pltpu.VMEM((2, rows, 128), jnp.float32),
            pltpu.VMEM((GROUP * 2 * rows, 2 * (offs - 1) * pairs), jnp.bfloat16),
            pltpu.VMEM((GROUP * 2 * rows, 2 * pairs), jnp.bfloat16),
            dma, dma((PIECES,)), dma((PIECES,)), dma((2, PIECES)), dma((PIECES,)), dma((3, 2)), dma((2, 2, 2)),
            regular, regular, dma((2,)), dma((2,)), dma, dma, dma((2,)), dma((2,)),
        ],
        compiler_params=pltpu.CompilerParams(collective_id=0, has_side_effects=True),
        name="noise_map",
    )(parts, pick_bins, path_cells, coarse, fine)


def solution(mesh):
    return jax.shard_map(
        on_device,
        mesh=mesh,
        in_specs=(
            P("sta", None, "per"),
            P(None, ("sta", "per"), None),
            P(("sta", "per"), None, None),
        ),
        out_specs=P("per", "sta", None),
        check_vma=False,
    )
```

```python
import functools
import math

import jax
import jax.numpy as jnp
import numpy as np
from jax import lax
from jax.experimental import pallas as pl
from jax.experimental.pallas import tpu as pltpu
from jax.sharding import PartitionSpec as P

FREQ = 8192
NLAG = 128
COARSE = 128
CHUNK = 512
PIECES = 2
GROUP = 16
MESH = pl.DeviceIdType.MESH


def angle_tables(per_count):
    lag = np.arange(NLAG, dtype=np.int64) - NLAG // 2
    coarse = np.arange(FREQ // COARSE, dtype=np.int64) * COARSE
    fine = np.arange(COARSE, dtype=np.int64)
    out = []
    for bins, scale in ((coarse, FREQ ** -0.5), (fine, 1.0)):
        turned = (bins[:, None] * lag[None, :]) % (2 * FREQ)
        phase = turned.astype(np.float64) * (math.pi / FREQ)
        out.append(np.stack([np.cos(phase), np.sin(phase)]).astype(np.float32) * np.float32(scale))
    coarse_table, fine_table = out
    coarse_table = coarse_table.reshape(2, per_count, -1, NLAG).transpose(1, 0, 2, 3)
    return coarse_table, fine_table


def build_table(coarse_ref, fine_ref, table_ref, per_place):
    band = table_ref.shape[1]

    def one(step, carry):
        c = coarse_ref[per_place, 0, pl.ds(step, 1), :]
        s = coarse_ref[per_place, 1, pl.ds(step, 1), :]
        rows = pl.ds(pl.multiple_of(step * COARSE, COARSE), COARSE)
        fc = fine_ref[0]
        fs = fine_ref[1]
        table_ref[0, rows, :] = (c * fc - s * fs).astype(jnp.bfloat16)
        table_ref[1, rows, :] = (-(s * fc + c * fs)).astype(jnp.bfloat16)
        return carry

    lax.fori_loop(0, band // COARSE, one, 0)


def correlate_into(acc, resident, visiting, table_ref, start, stop):
    count = resident.shape[1]
    if start == 0:
        acc[...] = jnp.zeros_like(acc)

    def one(step, carry):
        cols = pl.ds(pl.multiple_of(step * CHUNK, CHUNK), CHUNK)
        rre = resident[0, :, cols].astype(jnp.float32)
        rim = resident[1, :, cols].astype(jnp.float32)
        vre = visiting[0, :, cols].astype(jnp.float32)
        vim = visiting[1, :, cols].astype(jnp.float32)
        real, imag = [], []
        for i in range(count):
            a = rre[i:i + 1]
            b = rim[i:i + 1]
            real.append((a * vre + b * vim).astype(jnp.bfloat16))
            imag.append((b * vre - a * vim).astype(jnp.bfloat16))
        real = jnp.concatenate(real, axis=0)
        imag = jnp.concatenate(imag, axis=0)
        acc[...] += jnp.dot(real, table_ref[0, cols, :], preferred_element_type=jnp.float32) + jnp.dot(
            imag, table_ref[1, cols, :], preferred_element_type=jnp.float32
        )
        return carry

    lax.fori_loop(start // CHUNK, stop // CHUNK, one, 0)


def take_picks(acc, bins, is_own):
    turned = acc.T
    periods, pairs = bins.shape
    lag = lax.broadcasted_iota(jnp.int32, turned.shape, 0)
    rows = []
    for p in range(periods):
        rows.append(jnp.sum(jnp.where(lag == bins[p:p + 1], turned, 0.0), axis=0, keepdims=True))
    got = jnp.concatenate(rows, axis=0)
    if is_own:
        side = int(math.isqrt(pairs))
        place = lax.broadcasted_iota(jnp.int32, got.shape, 1)
        got = jnp.where(place // side == place % side, 0.0, got)
    return got


def kernel(sta_count, offs, parts_ref, bins_ref, cells_ref, coarse_ref, fine_ref, out_ref,
           blocks, all_bins, all_cells, table, accs, picks, peer_picks, spread, chip_landed, landed, outer_landed, edge_own, edge_mate, lhs_first, lhs,
           own_sem, near_send, near_recv, far_send, far_recv, index_send, index_recv, row_sem, col_sem,
           pick_send, pick_recv, chip_send, chip_recv, send_sem, recv_sem, outer_send, outer_recv, edge_send, edge_recv):
    sta = lax.axis_index("sta")
    per = lax.axis_index("per")
    even = lax.rem(sta, 2) == 0
    count = blocks.shape[2]
    band = blocks.shape[3]
    pairs = count * count
    piece = band // PIECES

    def around(step):
        return lax.rem(sta + (step + sta_count), sta_count)

    def digit_peers(stride):
        place = lax.rem(sta // stride, 4)
        return [sta + stride * (lax.rem(place + step, 4) - place) for step in (1, 2, 3)]

    def signal(sem, there, half):
        pl.semaphore_signal(sem, inc=1, device_id=(there, half), device_id_type=MESH)

    barrier = pltpu.get_barrier_semaphore()
    signal(barrier, sta, 1 - per)
    for step in (1, -1, 2, -2):
        signal(barrier, around(step), per)
    for step in (2, -2):
        signal(barrier, around(step), 1 - per)
    for stride in (1, 4, 16):
        for there in digit_peers(stride):
            signal(barrier, there, per)

    own = pltpu.make_async_copy(parts_ref, blocks.at[0], own_sem)
    own.start()
    own.wait()
    pl.semaphore_wait(barrier, 16)

    def copy(src, dst, send, recv, there, half):
        return pltpu.make_async_remote_copy(
            src_ref=src, dst_ref=dst, send_sem=send, recv_sem=recv, device_id=(there, half), device_id_type=MESH)

    def index_copies(there, half, slot, sems):
        return [copy(bins_ref, all_bins.at[slot, per], index_send.at[sems, 0], index_recv.at[slot, per, 0], there, half),
                copy(cells_ref, all_cells.at[slot, per], index_send.at[sems, 1], index_recv.at[slot, per, 1], there, half)]

    def cut(slot, number):
        return blocks.at[slot, :, :, pl.ds(number * piece, piece)]

    for c in index_copies(sta, 1 - per, 0, 0):
        c.start()
    near = [copy(cut(0, n), cut(1, n), near_send.at[n], near_recv.at[n], around(1), per) for n in range(PIECES)]
    back = [copy(cut(0, n), cut(2, n), far_send.at[0, n], far_recv.at[n], around(-2), per) for n in range(PIECES)]
    along = [copy(cut(1, n), cut(2, n), far_send.at[1, n], far_recv.at[n], around(1), per) for n in range(PIECES)]
    for n in range(PIECES):
        near[n].start()

        @pl.when(even)
        def _():
            back[n].start()

    @pl.when(even)
    def _():
        for half, sems in ((per, 1), (1 - per, 2)):
            for c in index_copies(around(-2), half, 1, sems):
                c.start()

    for there in digit_peers(16):
        signal(row_sem, there, per)

    build_table(coarse_ref, fine_ref, table, per)
    correlate_into(accs.at[0], blocks.at[0], blocks.at[0], table, 0, band)

    pl.semaphore_wait(row_sem, 3)
    for there in digit_peers(4):
        signal(col_sem, there, per)

    all_bins[0, per] = bins_ref[...]
    all_cells[0, per] = cells_ref[...]
    for ref, kind in ((bins_ref, 0), (cells_ref, 1)):
        pltpu.make_async_copy(ref, ref, index_recv.at[0, 1 - per, kind]).wait()
        pltpu.make_async_copy(ref, ref, index_send.at[0, kind]).wait()

    far_set = jnp.where(even, 1, 0)
    halves, residents = all_bins.shape[1], all_bins.shape[3]
    spots = [(h, i) for h in range(halves) for i in range(residents)]

    def bins_of(k):
        cols = slice(k * count, (k + 1) * count)
        which = far_set if k == offs - 1 else 0
        return jnp.concatenate([all_bins[which, h, :, i, cols] for h, i in spots], axis=1)

    def cells_of(k):
        cols = slice(k * count, (k + 1) * count)
        which = far_set if k == offs - 1 else 0
        return jnp.concatenate([all_cells[which, h, i, :, cols] for h, i in spots], axis=1)

    half = picks.shape[1]

    def pick(k):
        got = take_picks(accs[k], bins_of(k), k == 0)
        picks[0, :, k * pairs:(k + 1) * pairs] = got[:half]
        picks[1, :, k * pairs:(k + 1) * pairs] = got[half:]

    pick(0)
    for n in range(PIECES):
        near[n].wait_recv()

        @pl.when(even)
        def _():
            along[n].start()

        correlate_into(accs.at[1], blocks.at[0], blocks.at[1], table, n * piece, (n + 1) * piece)
    pick(1)

    def trade(number, start, stop):
        lanes = pl.ds(start, stop - start)
        return copy(picks.at[1 - per, :, lanes], peer_picks.at[:, lanes], pick_send.at[number], pick_recv.at[number],
                    sta, 1 - per)

    split = (offs - 1) * pairs
    first_trade = trade(0, 0, split)
    first_trade.start()
    resident = blocks.at[jnp.where(even, 2, 0)]
    visiting = blocks.at[jnp.where(even, 0, 2)]
    for n in range(PIECES):
        back[n].wait_recv()
        correlate_into(accs.at[2], resident, visiting, table, n * piece, (n + 1) * piece)

    @pl.when(even)
    def _():
        for half in range(2):
            for ref, kind in ((bins_ref, 0), (cells_ref, 1)):
                pltpu.make_async_copy(ref, ref, index_recv.at[1, half, kind]).wait()
                pltpu.make_async_copy(ref, ref, index_send.at[1 + half, kind]).wait()

    pick(2)
    last_trade = trade(1, split, offs * pairs)
    last_trade.start()
    pl.semaphore_wait(col_sem, 3)

    rows = 2 * half

    def ends_of(ks):
        cell = jnp.concatenate([cells_of(k) for k in ks], axis=1)
        row = cell // 128
        col = cell % 128
        row = jnp.concatenate([row[0:1], row[1:2]], axis=1)
        col = jnp.concatenate([col[0:1], col[1:2]], axis=1)
        hot = (lax.broadcasted_iota(jnp.int32, (128, col.shape[1]), 0) == col).astype(jnp.bfloat16)
        return jnp.broadcast_to(row, (2 * rows, row.shape[1])), hot

    def values(start, stop):
        total = picks[per, :, start:stop] + peer_picks[:, start:stop]
        both = jnp.concatenate([total, total * total], axis=0)
        high = both.astype(jnp.bfloat16).astype(jnp.float32)
        vals = jnp.concatenate([high, both - high], axis=0)
        return jnp.concatenate([vals, vals], axis=1)

    core = lax.rem(sta, 2)
    mates = [sta + 1 - 2 * core, sta]
    chips = sta_count // 2
    groups = list(reversed(range(0, chips, GROUP)))

    def add_up(lhs_ref, which, first, group, row, vals, hot):
        for r in range(group):
            wanted = lax.rem(mates[which] + 2 * (first + r), sta_count)
            lhs_ref[r * 2 * rows:(r + 1) * 2 * rows, :] = jnp.where(row == wanted, vals, 0.0).astype(jnp.bfloat16)
        grid = lax.dot_general(lhs_ref[...], hot, (((1,), (1,)), ((), ())), preferred_element_type=jnp.float32)
        grid = grid.reshape(group, 2, rows, 128)
        return grid[:, 0] + grid[:, 1]

    row, hot = ends_of(range(offs - 1))
    first_trade.wait()
    vals = values(0, split)
    for which in range(2):
        for first in groups:
            spread[which, first:first + GROUP] = add_up(lhs_first, which, first, GROUP, row, vals, hot)
    row, hot = ends_of([offs - 1])
    last_trade.wait()
    vals = values(split, offs * pairs)
    to_mate = []
    for n, first in enumerate(groups):
        spread[0, first:first + GROUP] += add_up(lhs, 0, first, GROUP, row, vals, hot)
        span = pl.ds(first, GROUP)
        to_mate.append(copy(spread.at[0, span], chip_landed.at[span], chip_send.at[n], chip_recv.at[n], mates[0], per))
        to_mate[n].start()
    for n, first in enumerate(groups):
        part = add_up(lhs, 1, first, GROUP, row, vals, hot)
        to_mate[n].wait_recv()
        spread[1, first:first + GROUP] += part + chip_landed[first:first + GROUP]

        def send_outer(step, carry):
            there = around(2 * step + 2 * core - 1)
            copy(spread.at[1, step], outer_landed.at[step], outer_send, outer_recv, there, per).start()
            return carry

        def send(step, carry):
            copy(spread.at[1, step], landed.at[step - 1], send_sem, recv_sem, around(2 * step), per).start()
            return carry

        lax.fori_loop(max(first, 1), first + GROUP, send, 0)
        lax.fori_loop(first, first + GROUP, send_outer, 0)
    for c in to_mate:
        c.wait_send()

    for n in range(PIECES):
        near[n].wait_send()

        @pl.when(even)
        def _():
            back[n].wait_send()
            along[n].wait_send()

    pltpu.make_async_copy(landed, landed, recv_sem).wait()
    edge_own[...] = spread[1, 0] + jnp.sum(landed[...], axis=0)
    to_edge = copy(edge_own, edge_mate, edge_send, edge_recv, mates[0], per)
    to_edge.start()
    mine = edge_own[...]
    lane = lax.broadcasted_iota(jnp.int32, mine.shape, 1)
    before_col = jnp.where(lane == 0, 0.0, pltpu.roll(mine, 1, 1))
    after_col = jnp.where(lane == 127, 0.0, pltpu.roll(mine, 127, 1))
    pltpu.make_async_copy(outer_landed, outer_landed, outer_recv).wait()
    outer = jnp.sum(outer_landed[...], axis=0)
    to_edge.wait()
    mate = edge_mate[...]
    before = jnp.where(sta == 0, 0.0, jnp.where(even, outer, mate))
    after = jnp.where(sta == sta_count - 1, 0.0, jnp.where(even, mate, outer))
    grad_rows = (after[:half] - before[:half]) * 0.5
    grad_cols = (after_col[:half] - before_col[:half]) * 0.5
    amp = 1.0 + mine[half:]
    laplace = ((1.0 + after[half:]) + (1.0 + before[half:]) + (1.0 + after_col[half:])
               + (1.0 + before_col[half:]) - 4.0 * amp)
    period = per * half + lax.broadcasted_iota(jnp.int32, laplace.shape, 0)
    weight = 1.0 / (1.0 + period.astype(jnp.float32))
    result = grad_rows * grad_rows + grad_cols * grad_cols - weight * laplace / amp
    out_ref[...] = result[:, None, :]
    pltpu.make_async_copy(landed, landed, send_sem).wait()
    pltpu.make_async_copy(outer_landed, outer_landed, outer_send).wait()


def on_device(spectra, pick_bins, path_cells):
    per_count = lax.axis_size("per")
    sta_count = lax.axis_size("sta")
    count, _, band = spectra.shape
    pairs = count * count
    periods = pick_bins.shape[0]
    offs = pick_bins.shape[2] // count
    parts = jnp.transpose(spectra, (1, 0, 2))
    coarse, fine = angle_tables(per_count)
    local = periods // per_count
    rows = 2 * local
    vmem = pl.BlockSpec(memory_space=pltpu.VMEM)
    dma = pltpu.SemaphoreType.DMA
    regular = pltpu.SemaphoreType.REGULAR
    return pl.pallas_call(
        functools.partial(kernel, sta_count, offs),
        out_shape=jax.ShapeDtypeStruct((local, 1, 128), jnp.float32),
        in_specs=[pl.BlockSpec(memory_space=pl.ANY)] + [vmem] * 4,
        out_specs=vmem,
        scratch_shapes=[
            pltpu.VMEM((3,) + parts.shape, parts.dtype),
            pltpu.VMEM((2, per_count) + pick_bins.shape, jnp.int32),
            pltpu.VMEM((2, per_count) + path_cells.shape, jnp.int32),
            pltpu.VMEM((2, band, NLAG), jnp.bfloat16),
            pltpu.VMEM((offs, pairs, NLAG), jnp.float32),
            pltpu.VMEM((per_count, local, offs * pairs), jnp.float32),
            pltpu.VMEM((local, offs * pairs), jnp.float32),
            pltpu.VMEM((2, sta_count // 2, rows, 128), jnp.float32),
            pltpu.VMEM((sta_count // 2, rows, 128), jnp.float32),
            pltpu.VMEM((sta_count // 2 - 1, rows, 128), jnp.float32),
            pltpu.VMEM((sta_count // 2, rows, 128), jnp.float32),
            pltpu.VMEM((rows, 128), jnp.float32),
            pltpu.VMEM((rows, 128), jnp.float32),
            pltpu.VMEM((GROUP * 2 * rows, 2 * (offs - 1) * pairs), jnp.bfloat16),
            pltpu.VMEM((GROUP * 2 * rows, 2 * pairs), jnp.bfloat16),
            dma, dma((PIECES,)), dma((PIECES,)), dma((2, PIECES)), dma((PIECES,)), dma((3, 2)), dma((2, 2, 2)),
            regular, regular, dma((2,)), dma((2,)), dma((2,)), dma((2,)), dma, dma, dma, dma, dma, dma,
        ],
        compiler_params=pltpu.CompilerParams(collective_id=0, has_side_effects=True),
        name="noise_map",
    )(parts, pick_bins, path_cells, coarse, fine)


def solution(mesh):
    return jax.shard_map(
        on_device,
        mesh=mesh,
        in_specs=(
            P("sta", None, "per"),
            P(None, ("sta", "per"), None),
            P(("sta", "per"), None, None),
        ),
        out_specs=P("per", "sta", None),
        check_vma=False,
    )
```

```python
import functools
import math

import jax
import jax.numpy as jnp
import numpy as np
from jax import lax
from jax.experimental import pallas as pl
from jax.experimental.pallas import tpu as pltpu
from jax.sharding import PartitionSpec as P

FREQ = 8192
NLAG = 128
COARSE = 128
CHUNK = 1024
PIECES = 2
GROUP = 16
MESH = pl.DeviceIdType.MESH


def angle_tables(per_count):
    lag = np.arange(NLAG, dtype=np.int64) - NLAG // 2
    coarse = np.arange(FREQ // COARSE, dtype=np.int64) * COARSE
    fine = np.arange(COARSE, dtype=np.int64)
    out = []
    for bins, scale in ((coarse, FREQ ** -0.5), (fine, 1.0)):
        turned = (bins[:, None] * lag[None, :]) % (2 * FREQ)
        phase = turned.astype(np.float64) * (math.pi / FREQ)
        out.append(np.stack([np.cos(phase), np.sin(phase)]).astype(np.float32) * np.float32(scale))
    coarse_table, fine_table = out
    coarse_table = coarse_table.reshape(2, per_count, -1, NLAG).transpose(1, 0, 2, 3)
    return coarse_table, fine_table


def build_table(coarse_ref, fine_ref, table_ref, per_place):
    band = table_ref.shape[1]

    def one(step, carry):
        c = coarse_ref[per_place, 0, pl.ds(step, 1), :]
        s = coarse_ref[per_place, 1, pl.ds(step, 1), :]
        rows = pl.ds(pl.multiple_of(step * COARSE, COARSE), COARSE)
        fc = fine_ref[0]
        fs = fine_ref[1]
        table_ref[0, rows, :] = (c * fc - s * fs).astype(jnp.bfloat16)
        table_ref[1, rows, :] = (-(s * fc + c * fs)).astype(jnp.bfloat16)
        return carry

    lax.fori_loop(0, band // COARSE, one, 0)


def correlate_into(acc, resident, visiting, table_ref, start, stop):
    count = resident.shape[1]
    if start == 0:
        acc[...] = jnp.zeros_like(acc)

    def one(step, carry):
        cols = pl.ds(pl.multiple_of(step * CHUNK, CHUNK), CHUNK)
        rre = resident[0, :, cols].astype(jnp.float32)
        rim = resident[1, :, cols].astype(jnp.float32)
        vre = visiting[0, :, cols].astype(jnp.float32)
        vim = visiting[1, :, cols].astype(jnp.float32)
        real, imag = [], []
        for i in range(count):
            a = rre[i:i + 1]
            b = rim[i:i + 1]
            real.append((a * vre + b * vim).astype(jnp.bfloat16))
            imag.append((b * vre - a * vim).astype(jnp.bfloat16))
        real = jnp.concatenate(real, axis=0)
        imag = jnp.concatenate(imag, axis=0)
        acc[...] += jnp.dot(real, table_ref[0, cols, :], preferred_element_type=jnp.float32) + jnp.dot(
            imag, table_ref[1, cols, :], preferred_element_type=jnp.float32
        )
        return carry

    lax.fori_loop(start // CHUNK, stop // CHUNK, one, 0)


def take_picks(acc, bins, is_own):
    turned = acc.T
    periods, pairs = bins.shape
    lag = lax.broadcasted_iota(jnp.int32, turned.shape, 0)
    rows = []
    for p in range(periods):
        rows.append(jnp.sum(jnp.where(lag == bins[p:p + 1], turned, 0.0), axis=0, keepdims=True))
    got = jnp.concatenate(rows, axis=0)
    if is_own:
        side = int(math.isqrt(pairs))
        place = lax.broadcasted_iota(jnp.int32, got.shape, 1)
        got = jnp.where(place // side == place % side, 0.0, got)
    return got


def kernel(sta_count, offs, parts_ref, bins_ref, cells_ref, coarse_ref, fine_ref, out_ref,
           blocks, all_bins, all_cells, table, accs, picks, peer_picks, spread, chip_landed, landed, outer_landed, edge_own, edge_mate, lhs_first, lhs,
           own_sem, near_send, near_recv, far_send, far_recv, index_send, index_recv, row_sem, col_sem,
           pick_send, pick_recv, chip_send, chip_recv, send_sem, recv_sem, outer_send, outer_recv, edge_send, edge_recv):
    sta = lax.axis_index("sta")
    per = lax.axis_index("per")
    even = lax.rem(sta, 2) == 0
    count = blocks.shape[2]
    band = blocks.shape[3]
    pairs = count * count
    piece = band // PIECES

    def around(step):
        return lax.rem(sta + (step + sta_count), sta_count)

    def digit_peers(stride):
        place = lax.rem(sta // stride, 4)
        return [sta + stride * (lax.rem(place + step, 4) - place) for step in (1, 2, 3)]

    def signal(sem, there, half):
        pl.semaphore_signal(sem, inc=1, device_id=(there, half), device_id_type=MESH)

    barrier = pltpu.get_barrier_semaphore()
    signal(barrier, sta, 1 - per)
    for step in (1, -1, 2, -2):
        signal(barrier, around(step), per)
    for step in (2, -2):
        signal(barrier, around(step), 1 - per)
    for stride in (1, 4, 16):
        for there in digit_peers(stride):
            signal(barrier, there, per)

    own = pltpu.make_async_copy(parts_ref, blocks.at[0], own_sem)
    own.start()
    own.wait()
    pl.semaphore_wait(barrier, 16)

    def copy(src, dst, send, recv, there, half):
        return pltpu.make_async_remote_copy(
            src_ref=src, dst_ref=dst, send_sem=send, recv_sem=recv, device_id=(there, half), device_id_type=MESH)

    def index_copies(there, half, slot, sems):
        return [copy(bins_ref, all_bins.at[slot, per], index_send.at[sems, 0], index_recv.at[slot, per, 0], there, half),
                copy(cells_ref, all_cells.at[slot, per], index_send.at[sems, 1], index_recv.at[slot, per, 1], there, half)]

    def cut(slot, number):
        return blocks.at[slot, :, :, pl.ds(number * piece, piece)]

    for c in index_copies(sta, 1 - per, 0, 0):
        c.start()
    near = [copy(cut(0, n), cut(1, n), near_send.at[n], near_recv.at[n], around(1), per) for n in range(PIECES)]
    back = [copy(cut(0, n), cut(2, n), far_send.at[0, n], far_recv.at[n], around(-2), per) for n in range(PIECES)]
    along = [copy(cut(1, n), cut(2, n), far_send.at[1, n], far_recv.at[n], around(1), per) for n in range(PIECES)]
    for n in range(PIECES):
        near[n].start()

        @pl.when(even)
        def _():
            back[n].start()

    @pl.when(even)
    def _():
        for half, sems in ((per, 1), (1 - per, 2)):
            for c in index_copies(around(-2), half, 1, sems):
                c.start()

    for there in digit_peers(16):
        signal(row_sem, there, per)

    build_table(coarse_ref, fine_ref, table, per)
    correlate_into(accs.at[0], blocks.at[0], blocks.at[0], table, 0, band)

    pl.semaphore_wait(row_sem, 3)
    for there in digit_peers(4):
        signal(col_sem, there, per)

    all_bins[0, per] = bins_ref[...]
    all_cells[0, per] = cells_ref[...]
    for ref, kind in ((bins_ref, 0), (cells_ref, 1)):
        pltpu.make_async_copy(ref, ref, index_recv.at[0, 1 - per, kind]).wait()
        pltpu.make_async_copy(ref, ref, index_send.at[0, kind]).wait()

    far_set = jnp.where(even, 1, 0)
    halves, residents = all_bins.shape[1], all_bins.shape[3]
    spots = [(h, i) for h in range(halves) for i in range(residents)]

    def bins_of(k):
        cols = slice(k * count, (k + 1) * count)
        which = far_set if k == offs - 1 else 0
        return jnp.concatenate([all_bins[which, h, :, i, cols] for h, i in spots], axis=1)

    def cells_of(k):
        cols = slice(k * count, (k + 1) * count)
        which = far_set if k == offs - 1 else 0
        return jnp.concatenate([all_cells[which, h, i, :, cols] for h, i in spots], axis=1)

    half = picks.shape[1]

    def pick(k):
        got = take_picks(accs[k], bins_of(k), k == 0)
        picks[0, :, k * pairs:(k + 1) * pairs] = got[:half]
        picks[1, :, k * pairs:(k + 1) * pairs] = got[half:]

    pick(0)
    for n in range(PIECES):
        near[n].wait_recv()

        @pl.when(even)
        def _():
            along[n].start()

        correlate_into(accs.at[1], blocks.at[0], blocks.at[1], table, n * piece, (n + 1) * piece)
    pick(1)

    def trade(number, start, stop):
        lanes = pl.ds(start, stop - start)
        return copy(picks.at[1 - per, :, lanes], peer_picks.at[:, lanes], pick_send.at[number], pick_recv.at[number],
                    sta, 1 - per)

    split = (offs - 1) * pairs
    first_trade = trade(0, 0, split)
    first_trade.start()
    resident = blocks.at[jnp.where(even, 2, 0)]
    visiting = blocks.at[jnp.where(even, 0, 2)]
    for n in range(PIECES):
        back[n].wait_recv()
        correlate_into(accs.at[2], resident, visiting, table, n * piece, (n + 1) * piece)

    @pl.when(even)
    def _():
        for half in range(2):
            for ref, kind in ((bins_ref, 0), (cells_ref, 1)):
                pltpu.make_async_copy(ref, ref, index_recv.at[1, half, kind]).wait()
                pltpu.make_async_copy(ref, ref, index_send.at[1 + half, kind]).wait()

    pick(2)
    last_trade = trade(1, split, offs * pairs)
    last_trade.start()
    pl.semaphore_wait(col_sem, 3)

    rows = 2 * half

    def ends_of(ks):
        cell = jnp.concatenate([cells_of(k) for k in ks], axis=1)
        row = cell // 128
        col = cell % 128
        row = jnp.concatenate([row[0:1], row[1:2]], axis=1)
        col = jnp.concatenate([col[0:1], col[1:2]], axis=1)
        hot = (lax.broadcasted_iota(jnp.int32, (128, col.shape[1]), 0) == col).astype(jnp.bfloat16)
        return jnp.broadcast_to(row, (2 * rows, row.shape[1])), hot

    def values(start, stop):
        total = picks[per, :, start:stop] + peer_picks[:, start:stop]
        both = jnp.concatenate([total, total * total], axis=0)
        high = both.astype(jnp.bfloat16).astype(jnp.float32)
        vals = jnp.concatenate([high, both - high], axis=0)
        return jnp.concatenate([vals, vals], axis=1)

    core = lax.rem(sta, 2)
    mates = [sta + 1 - 2 * core, sta]
    chips = sta_count // 2
    groups = list(reversed(range(0, chips, GROUP)))

    def add_up(lhs_ref, which, first, group, row, vals, hot):
        for r in range(group):
            wanted = lax.rem(mates[which] + 2 * (first + r), sta_count)
            lhs_ref[r * 2 * rows:(r + 1) * 2 * rows, :] = jnp.where(row == wanted, vals, 0.0).astype(jnp.bfloat16)
        grid = lax.dot_general(lhs_ref[...], hot, (((1,), (1,)), ((), ())), preferred_element_type=jnp.float32)
        grid = grid.reshape(group, 2, rows, 128)
        return grid[:, 0] + grid[:, 1]

    row, hot = ends_of(range(offs - 1))
    first_trade.wait()
    vals = values(0, split)
    for which in range(2):
        for first in groups:
            spread[which, first:first + GROUP] = add_up(lhs_first, which, first, GROUP, row, vals, hot)
    row, hot = ends_of([offs - 1])
    last_trade.wait()
    vals = values(split, offs * pairs)
    to_mate = []
    for n, first in enumerate(groups):
        spread[0, first:first + GROUP] += add_up(lhs, 0, first, GROUP, row, vals, hot)
        span = pl.ds(first, GROUP)
        to_mate.append(copy(spread.at[0, span], chip_landed.at[span], chip_send.at[n], chip_recv.at[n], mates[0], per))
        to_mate[n].start()
    for n, first in enumerate(groups):
        part = add_up(lhs, 1, first, GROUP, row, vals, hot)
        to_mate[n].wait_recv()
        spread[1, first:first + GROUP] += part + chip_landed[first:first + GROUP]

        def send_outer(step, carry):
            there = around(2 * step + 2 * core - 1)
            copy(spread.at[1, step], outer_landed.at[step], outer_send, outer_recv, there, per).start()
            return carry

        def send(step, carry):
            copy(spread.at[1, step], landed.at[step - 1], send_sem, recv_sem, around(2 * step), per).start()
            return carry

        lax.fori_loop(max(first, 1), first + GROUP, send, 0)
        lax.fori_loop(first, first + GROUP, send_outer, 0)
    for c in to_mate:
        c.wait_send()

    for n in range(PIECES):
        near[n].wait_send()

        @pl.when(even)
        def _():
            back[n].wait_send()
            along[n].wait_send()

    pltpu.make_async_copy(landed, landed, recv_sem).wait()
    edge_own[...] = spread[1, 0] + jnp.sum(landed[...], axis=0)
    to_edge = copy(edge_own, edge_mate, edge_send, edge_recv, mates[0], per)
    to_edge.start()
    mine = edge_own[...]
    lane = lax.broadcasted_iota(jnp.int32, mine.shape, 1)
    before_col = jnp.where(lane == 0, 0.0, pltpu.roll(mine, 1, 1))
    after_col = jnp.where(lane == 127, 0.0, pltpu.roll(mine, 127, 1))
    pltpu.make_async_copy(outer_landed, outer_landed, outer_recv).wait()
    outer = jnp.sum(outer_landed[...], axis=0)
    to_edge.wait()
    mate = edge_mate[...]
    before = jnp.where(sta == 0, 0.0, jnp.where(even, outer, mate))
    after = jnp.where(sta == sta_count - 1, 0.0, jnp.where(even, mate, outer))
    grad_rows = (after[:half] - before[:half]) * 0.5
    grad_cols = (after_col[:half] - before_col[:half]) * 0.5
    amp = 1.0 + mine[half:]
    laplace = ((1.0 + after[half:]) + (1.0 + before[half:]) + (1.0 + after_col[half:])
               + (1.0 + before_col[half:]) - 4.0 * amp)
    period = per * half + lax.broadcasted_iota(jnp.int32, laplace.shape, 0)
    weight = 1.0 / (1.0 + period.astype(jnp.float32))
    result = grad_rows * grad_rows + grad_cols * grad_cols - weight * laplace / amp
    out_ref[...] = result[:, None, :]
    pltpu.make_async_copy(landed, landed, send_sem).wait()
    pltpu.make_async_copy(outer_landed, outer_landed, outer_send).wait()


def on_device(spectra, pick_bins, path_cells):
    per_count = lax.axis_size("per")
    sta_count = lax.axis_size("sta")
    count, _, band = spectra.shape
    pairs = count * count
    periods = pick_bins.shape[0]
    offs = pick_bins.shape[2] // count
    parts = jnp.transpose(spectra, (1, 0, 2))
    coarse, fine = angle_tables(per_count)
    local = periods // per_count
    rows = 2 * local
    vmem = pl.BlockSpec(memory_space=pltpu.VMEM)
    dma = pltpu.SemaphoreType.DMA
    regular = pltpu.SemaphoreType.REGULAR
    return pl.pallas_call(
        functools.partial(kernel, sta_count, offs),
        out_shape=jax.ShapeDtypeStruct((local, 1, 128), jnp.float32),
        in_specs=[pl.BlockSpec(memory_space=pl.ANY)] + [vmem] * 4,
        out_specs=vmem,
        scratch_shapes=[
            pltpu.VMEM((3,) + parts.shape, parts.dtype),
            pltpu.VMEM((2, per_count) + pick_bins.shape, jnp.int32),
            pltpu.VMEM((2, per_count) + path_cells.shape, jnp.int32),
            pltpu.VMEM((2, band, NLAG), jnp.bfloat16),
            pltpu.VMEM((offs, pairs, NLAG), jnp.float32),
            pltpu.VMEM((per_count, local, offs * pairs), jnp.float32),
            pltpu.VMEM((local, offs * pairs), jnp.float32),
            pltpu.VMEM((2, sta_count // 2, rows, 128), jnp.float32),
            pltpu.VMEM((sta_count // 2, rows, 128), jnp.float32),
            pltpu.VMEM((sta_count // 2 - 1, rows, 128), jnp.float32),
            pltpu.VMEM((sta_count // 2, rows, 128), jnp.float32),
            pltpu.VMEM((rows, 128), jnp.float32),
            pltpu.VMEM((rows, 128), jnp.float32),
            pltpu.VMEM((GROUP * 2 * rows, 2 * (offs - 1) * pairs), jnp.bfloat16),
            pltpu.VMEM((GROUP * 2 * rows, 2 * pairs), jnp.bfloat16),
            dma, dma((PIECES,)), dma((PIECES,)), dma((2, PIECES)), dma((PIECES,)), dma((3, 2)), dma((2, 2, 2)),
            regular, regular, dma((2,)), dma((2,)), dma((2,)), dma((2,)), dma, dma, dma, dma, dma, dma,
        ],
        compiler_params=pltpu.CompilerParams(collective_id=0, has_side_effects=True),
        name="noise_map",
    )(parts, pick_bins, path_cells, coarse, fine)


def solution(mesh):
    return jax.shard_map(
        on_device,
        mesh=mesh,
        in_specs=(
            P("sta", None, "per"),
            P(None, ("sta", "per"), None),
            P(("sta", "per"), None, None),
        ),
        out_specs=P("per", "sta", None),
        check_vma=False,
    )
```
